256 devices in a mesh: sec: 16 (over z, core), term: 16 (over y, x).
Axes of the slice: x: 4, y: 4, z: 8, core: 2. Of those that a mesh axis runs over, the one named last changes fastest.
Arguments:
- psi: bfloat16 [16, 512, 512], P('sec'), may hold values from -6 to 6
- left_ops: bfloat16 [16, 96, 512, 512], P('sec', 'term'), may hold values from -0.078125 to 0.078125
- right_ops: bfloat16 [16, 96, 512, 512], P('sec', 'term'), may hold values from -0.078125 to 0.078125
- term_mask: int32 [16, 96], P('sec', 'term'), may hold values 0 or 1
- pair_src: int32 [16], P('sec'), may hold values from 0 to 15, each once
- pair_dst: int32 [16], P('sec'), may hold values from 0 to 15, each once
Outputs:
- sigma: bfloat16 [16, 512, 512], P('sec')
The draws below stay inside these ranges and needn't reach their ends.
Inputs may be any that keep to these rules, and one draw needn't show every extreme that they name: `pair_src`: each of the 16 sector blocks is the source of exactly one pair. `pair_dst`: each of the 16 sector blocks is the target of exactly one pair.
All inputs are finite; a program needn't handle non-finite values. No bound on the sum of `term_mask` on one device may be relied on, other than what follows from the above.
Results may differ from the reference program's by a relative error of at most 0.0065.
Values may be sent and summed in bfloat16 or wider, within the bound.
A program may use at most 64 MiB of HBM per device.

```python
import jax
import jax.numpy as jnp
from jax import lax

BLK = 512
NSEC = 16
TERMS = 96


def place_ends(drawn, own_key, low, top_value):
    longest = drawn.shape.index(max(drawn.shape))
    spots = []
    for shift in (0, 1):
        where = [jax.random.randint(jax.random.fold_in(own_key, axis), (), 0, length) for axis, length in enumerate(drawn.shape)]
        where[longest] = (where[longest] + shift) % drawn.shape[longest]
        spots.append(tuple(where))
    return drawn.at[spots[0]].set(low).at[spots[1]].set(top_value)


def levels(key, shape, shards, smallest, high):
    factor_of, own = 1.0, jax.random.fold_in(key, 6)
    for position, parts in shards:
        heights = jnp.exp(jax.random.uniform(jax.random.fold_in(own, position), (parts,), jnp.float32, smallest / len(shards), high / len(shards)))
        factor_of = factor_of * jnp.repeat(heights, shape[position] // parts).reshape([-1 if axis == position else 1 for axis in range(len(shape))])
    return factor_of


def centred(stream_key, extent, spread, reach, shards=(), held_as=jnp.bfloat16):
    result = spread * jax.random.normal(stream_key, extent, jnp.float32)
    if shards:
        result = result * levels(stream_key, extent, shards, -0.22, 0.18)
    return jnp.clip(result, -reach, reach).astype(held_as)


def setup_inputs(seed: int = 0) -> dict:
    streams_of = jax.random.split(jax.random.key(seed), 7)
    psi = centred(streams_of[0], (NSEC, BLK, BLK), 1.0, 6.0, ((0, 16),))
    left_ops = centred(streams_of[1], (NSEC, TERMS, BLK, BLK), (BLK * 12) ** -0.5, 0.078125, ((0, 16), (1, 16)))
    right_ops = centred(streams_of[2], (NSEC, TERMS, BLK, BLK), (BLK * 12) ** -0.5, 0.078125, ((0, 16), (1, 16)))
    term_mask = place_ends((jax.random.randint(streams_of[3], (NSEC, TERMS), 0, 2) < 1).astype(jnp.int32), jax.random.fold_in(streams_of[3], 1), 0, 1)
    pair_src = jax.random.permutation(streams_of[4], NSEC).astype(jnp.int32)
    pair_dst = jax.random.permutation(streams_of[5], NSEC).astype(jnp.int32)
    return {"psi": psi, "left_ops": left_ops, "right_ops": right_ops, "term_mask": term_mask, "pair_src": pair_src, "pair_dst": pair_dst}


def reference(psi, left_ops, right_ops, term_mask, pair_src, pair_dst):
    zero_block = jnp.zeros((BLK, BLK), jnp.float32)

    def pair_step(sigma_acc, index):
        source = pair_src[index]
        target = pair_dst[index]
        src_block = psi[source]
        dst_block = psi[target]

        def term_step(acc, term):
            def active(carry):
                fwd_acc, adj_acc = carry
                left = left_ops[index, term]
                right = right_ops[index, term]
                inner_fwd = jnp.dot(left, src_block, preferred_element_type=jnp.float32).astype(jnp.bfloat16)
                inner_adj = jnp.dot(left.T, dst_block, preferred_element_type=jnp.float32).astype(jnp.bfloat16)
                fwd_acc = fwd_acc + jnp.dot(inner_fwd, right.T, preferred_element_type=jnp.float32)
                adj_acc = adj_acc + jnp.dot(inner_adj, right, preferred_element_type=jnp.float32)
                return fwd_acc, adj_acc

            return lax.cond(term_mask[index, term] == 1, active, lambda carry: carry, acc), None

        (fwd, adj), _ = lax.scan(term_step, (zero_block, zero_block), jnp.arange(TERMS, dtype=jnp.int32))
        sigma_acc = sigma_acc.at[target].add(fwd)
        sigma_acc = sigma_acc.at[source].add(adj)
        return sigma_acc, None

    start = jnp.zeros((NSEC, BLK, BLK), jnp.float32)
    total, _ = lax.scan(pair_step, start, jnp.arange(NSEC, dtype=jnp.int32))
    return total.astype(jnp.bfloat16)
```

```python
import functools

import jax
import jax.numpy as jnp
from jax import lax
from jax.experimental import pallas as pl
from jax.experimental.pallas import tpu as pltpu
from jax.sharding import PartitionSpec as P

MESH = pl.DeviceIdType.MESH
F32, BF16 = jnp.float32, jnp.bfloat16


def remote(src, dst, send_sem, recv_sem, device):
    return pltpu.make_async_remote_copy(
        src_ref=src,
        dst_ref=dst,
        send_sem=send_sem,
        recv_sem=recv_sem,
        device_id=device,
        device_id_type=MESH,
    )


def wait_for(ref, sem):
    pltpu.make_async_copy(ref, ref, sem).wait()


def kernel(
    sizes,
    psi,
    left,
    right,
    mask,
    src,
    dst,
    out,
    left_v,
    right_v,
    column,
    handed,
    given,
    blocks,
    label,
    labels,
    label_p,
    total,
    part,
    arrived,
    rows_out,
    rows_in,
    mine_v,
    local_sem,
    send_sem,
    recv_sem,
):
    nsec, nterm, terms, order = sizes
    nz = nsec // 2
    rows = order // nterm
    s, t = lax.axis_index("sec"), lax.axis_index("term")
    z, c = s // 2, s % 2
    partner = {"sec": z * 2 + (1 - c)}

    def on_z(d):
        return {"sec": ((z + nz - d) % nz) * 2 + c}

    def on_term(j):
        return {"term": (t + j) % nterm}

    def row_block(index):
        return pl.ds(pl.multiple_of(index * rows, rows), rows)

    far_first = sorted(range(1, nz), key=lambda d: -min(d, nz - d))

    load_left = pltpu.make_async_copy(left.at[0], left_v, local_sem.at[0])
    load_right = pltpu.make_async_copy(right.at[0], right_v, local_sem.at[1])
    own = pltpu.make_async_copy(psi.at[0, row_block(t)], column.at[0], local_sem.at[2])
    own.start()

    label[0:8, :] = jnp.full((8, 128), src[0], jnp.int32).astype(F32)
    label[8:16, :] = jnp.full((8, 128), dst[0], jnp.int32).astype(F32)

    barrier = pltpu.get_barrier_semaphore()
    pl.semaphore_signal(barrier, inc=1, device_id=partner, device_id_type=MESH)
    for d in far_first:
        pl.semaphore_signal(barrier, inc=1, device_id=on_z(d), device_id_type=MESH)

    def greet(j, carry):
        pl.semaphore_signal(barrier, inc=1, device_id=on_term(j), device_id_type=MESH)
        return carry

    lax.fori_loop(1, nterm, greet, 0)
    pl.semaphore_wait(barrier, nz + nterm - 1)

    for d in far_first:
        remote(
            psi.at[0, row_block(t)], column.at[d], send_sem.at[0], recv_sem.at[0], on_z(d)
        ).start()
    remote(label, label_p, send_sem.at[1], recv_sem.at[1], partner).start()
    for d in far_first:
        remote(label, labels.at[d], send_sem.at[2], recv_sem.at[2], on_z(d)).start()
    load_left.start()
    load_right.start()

    def row_of(labels_row):
        return jnp.concatenate([labels_row] * (order // 128), axis=1)

    def owner(d):
        return (((z + d) % nz) * 2 + c).astype(F32)

    wait_for(label_p, recv_sem.at[1])
    own.wait()
    wait_for(column.at[pl.ds(1, nz - 1)], recv_sem.at[0])
    for which in range(2):
        wanted = row_of(label_p[8 * which : 8 * which + 1, :])

        def pick(d, value):
            return jnp.where(wanted == owner(d), column[d].astype(F32), value)

        value = jnp.zeros((rows, order), F32)
        for d in range(nz):
            value = pick(d, value)
        given[which] = value.astype(BF16)
        remote(
            given.at[which], handed.at[which], send_sem.at[3], recv_sem.at[3 + which], partner
        ).start()
    for which in range(2):
        wanted = (src, dst)[which][0]
        local = column[(wanted // 2 + nz - z) % nz]
        wait_for(handed.at[which], recv_sem.at[3 + which])
        blocks[which, row_block(t), :] = jnp.where(wanted % 2 == c, local, handed[which])

        def send(j, carry):
            remote(
                blocks.at[which, row_block(t)],
                blocks.at[which, row_block(t)],
                send_sem.at[5 + which],
                recv_sem.at[5 + which],
                on_term(j),
            ).start()
            return carry

        lax.fori_loop(1, nterm, send, 0)

    others = pl.ds(0, (nterm - 1) * rows)
    load_left.wait()
    load_right.wait()
    for which in range(2):
        wait_for(blocks.at[which, others], recv_sem.at[5 + which])
        total[which] = jnp.zeros((order, order), F32)

        def add_term(term, carry):
            active = jnp.where(mask[0, term] == 1, 1.0, 0.0).astype(F32)
            if which == 0:
                inner = jnp.dot(left_v[term], blocks[which], preferred_element_type=F32)
                outer_dims = (((1,), (1,)), ((), ()))
            else:
                inner = lax.dot_general(
                    left_v[term],
                    blocks[which],
                    (((0,), (0,)), ((), ())),
                    preferred_element_type=F32,
                )
                outer_dims = (((1,), (0,)), ((), ()))
            inner = (inner * active).astype(BF16)
            total[which] += lax.dot_general(
                inner, right_v[term], outer_dims, preferred_element_type=F32
            )
            return carry

        lax.fori_loop(0, terms, add_term, 0)
        part[which] = total[which].astype(BF16)

        def scatter(j, carry):
            remote(
                part.at[which, row_block((t + j) % nterm)],
                arrived.at[which, nterm - 1 - j],
                send_sem.at[7 + which],
                recv_sem.at[7 + which],
                on_term(j),
            ).start()
            return carry

        lax.fori_loop(1, nterm, scatter, 0)

    for which in range(2):
        wait_for(arrived.at[which, pl.ds(0, nterm - 1)], recv_sem.at[7 + which])
        summed = total[which, row_block(t), :]
        for j in range(nterm - 1):
            summed = summed + arrived[which, j].astype(F32)
        rows_out[which] = summed.astype(BF16)
        for d in far_first:
            remote(
                rows_out.at[which],
                rows_in.at[which, d],
                send_sem.at[9 + which],
                recv_sem.at[9 + which],
                on_z(d),
            ).start()

    wait_for(labels.at[pl.ds(1, nz - 1)], recv_sem.at[2])
    for which in range(2):
        wait_for(rows_in.at[which, pl.ds(1, nz - 1)], recv_sem.at[9 + which])

    def collected(sector):
        sector = sector.astype(F32)
        value = jnp.zeros((rows, order), F32)
        for d in range(nz):
            tags = label if d == 0 else labels.at[d]
            for which in range(2):
                tag = row_of(tags[8 * (1 - which) : 8 * (1 - which) + 1, :])
                rows_d = rows_out[which] if d == 0 else rows_in[which, d]
                value = value + jnp.where(tag == sector, rows_d.astype(F32), 0.0)
        return value

    given[2] = collected(z * 2 + (1 - c)).astype(BF16)
    remote(given.at[2], handed.at[2], send_sem.at[11], recv_sem.at[11], partner).start()
    value = collected(s)
    wait_for(handed.at[2], recv_sem.at[11])
    mine_v[...] = (value + handed[2].astype(F32)).astype(BF16)
    keep = pltpu.make_async_copy(mine_v, out.at[0, row_block(t)], local_sem.at[2])
    keep.start()

    def spread(j, carry):
        remote(
            mine_v, out.at[0, row_block(t)], send_sem.at[12], recv_sem.at[12], on_term(j)
        ).start()
        return carry

    lax.fori_loop(1, nterm, spread, 0)

    wait_for(column.at[pl.ds(1, nz - 1)], send_sem.at[0])
    wait_for(label, send_sem.at[1])
    wait_for(labels.at[pl.ds(1, nz - 1)], send_sem.at[2])
    wait_for(given.at[pl.ds(0, 2)], send_sem.at[3])
    for which in range(2):
        wait_for(blocks.at[which, others], send_sem.at[5 + which])
        wait_for(part.at[which, others], send_sem.at[7 + which])
        wait_for(rows_in.at[which, pl.ds(1, nz - 1)], send_sem.at[9 + which])
    wait_for(given.at[2], send_sem.at[11])
    keep.wait()
    wait_for(out.at[0, others], send_sem.at[12])
    wait_for(out.at[0, others], recv_sem.at[12])


def solution(mesh):
    nsec, nterm = mesh.shape["sec"], mesh.shape["term"]
    placed = (
        P("sec", None, None),
        P("sec", "term", None, None),
        P("sec", "term", None, None),
        P("sec", "term"),
        P("sec"),
        P("sec"),
    )

    def local(psi, left_ops, right_ops, term_mask, pair_src, pair_dst):
        order, terms = psi.shape[1], left_ops.shape[1]
        rows, nz = order // nterm, nsec // 2
        anywhere = pl.BlockSpec(memory_space=pl.ANY)
        scalars = pl.BlockSpec(memory_space=pltpu.SMEM)
        return pl.pallas_call(
            functools.partial(kernel, (nsec, nterm, terms, order)),
            out_shape=jax.ShapeDtypeStruct(psi.shape, BF16),
            in_specs=[anywhere] * 3 + [scalars] * 3,
            out_specs=anywhere,
            scratch_shapes=[
                pltpu.VMEM((terms, order, order), BF16),
                pltpu.VMEM((terms, order, order), BF16),
                pltpu.VMEM((nz, rows, order), BF16),
                pltpu.VMEM((3, rows, order), BF16),
                pltpu.VMEM((3, rows, order), BF16),
                pltpu.VMEM((2, order, order), BF16),
                pltpu.VMEM((16, 128), F32),
                pltpu.VMEM((nz, 16, 128), F32),
                pltpu.VMEM((16, 128), F32),
                pltpu.VMEM((2, order, order), F32),
                pltpu.VMEM((2, order, order), BF16),
                pltpu.VMEM((2, nterm, rows, order), BF16),
                pltpu.VMEM((2, rows, order), BF16),
                pltpu.VMEM((2, nz, rows, order), BF16),
                pltpu.VMEM((rows, order), BF16),
                pltpu.SemaphoreType.DMA((3,)),
                pltpu.SemaphoreType.DMA((13,)),
                pltpu.SemaphoreType.DMA((13,)),
            ],
            compiler_params=pltpu.CompilerParams(
                collective_id=0, has_side_effects=True, vmem_limit_bytes=48 * 1024 * 1024
            ),
        )(psi, left_ops, right_ops, term_mask, pair_src, pair_dst)

    return jax.shard_map(
        local, mesh=mesh, in_specs=placed, out_specs=P("sec", None, None), check_vma=False
    )
```

```python
import functools

import jax
import jax.numpy as jnp
from jax import lax
from jax.experimental import pallas as pl
from jax.experimental.pallas import tpu as pltpu
from jax.sharding import PartitionSpec as P

MESH = pl.DeviceIdType.MESH
F32, BF16 = jnp.float32, jnp.bfloat16


def remote(src, dst, send_sem, recv_sem, device):
    return pltpu.make_async_remote_copy(
        src_ref=src,
        dst_ref=dst,
        send_sem=send_sem,
        recv_sem=recv_sem,
        device_id=device,
        device_id_type=MESH,
    )


def wait_for(ref, sem):
    pltpu.make_async_copy(ref, ref, sem).wait()


def kernel(
    sizes,
    psi,
    left,
    right,
    mask,
    src,
    dst,
    out,
    left_v,
    right_v,
    column_a,
    column_b,
    handed,
    given,
    blocks,
    label,
    label_p,
    inner_v,
    total,
    part,
    arrived,
    sums,
    sums_p,
    leaving,
    landed,
    mine_v,
    mask_s,
    src_s,
    dst_s,
    local_sem,
    hand_send,
    hand_recv,
    column_send,
    column_recv,
    block_send,
    block_recv,
    part_send,
    part_recv,
    swap_send,
    swap_recv,
    land_send,
    land_recv,
    out_send,
    out_recv,
):
    nsec, nterm, terms, order = sizes
    column = (column_a, column_b)
    nz = nsec // 2
    rows = order // nterm
    wide = order // 2
    s, t = lax.axis_index("sec"), lax.axis_index("term")
    z, c = s // 2, s % 2
    partner = {"sec": z * 2 + (1 - c)}
    halves = [pl.ds(h * wide, wide) for h in range(2)]
    other_z = pl.ds(1, nz - 1)
    other_t = pl.ds(0, nterm - 1)
    other_rows = pl.ds(0, (nterm - 1) * rows)

    def on_z(d):
        return {"sec": ((z + nz - d) % nz) * 2 + c}

    def on_term(j):
        return {"term": (t + j) % nterm}

    def row_block(index):
        return pl.ds(pl.multiple_of(index * rows, rows), rows)

    def to_all_terms(make):
        def start(j, carry):
            make(j).start()
            return carry

        lax.fori_loop(1, nterm, start, 0)

    my_rows = row_block(t)
    far_first = sorted(range(1, nz), key=lambda d: -min(d, nz - d))

    scalars = [
        pltpu.make_async_copy(a, b, local_sem.at[3 + i])
        for i, (a, b) in enumerate(((mask, mask_s), (src, src_s), (dst, dst_s)))
    ]
    for copy in scalars:
        copy.start()
    own = [
        pltpu.make_async_copy(psi.at[0, my_rows, halves[h]], column[h].at[0], local_sem.at[1 + h])
        for h in range(2)
    ]
    for copy in own:
        copy.start()

    barrier = pltpu.get_barrier_semaphore()
    for d in far_first:
        pl.semaphore_signal(barrier, inc=1, device_id=on_z(d), device_id_type=MESH)
    pl.semaphore_signal(barrier, inc=1, device_id=partner, device_id_type=MESH)

    def greet(j, carry):
        pl.semaphore_signal(barrier, inc=1, device_id=on_term(j), device_id_type=MESH)
        return carry

    lax.fori_loop(1, nterm, greet, 0)
    for copy in scalars:
        copy.wait()
    ends = (src_s[0], dst_s[0])
    for which in range(2):
        label[8 * which : 8 * which + 8, :] = jnp.full((8, 128), ends[which], jnp.int32).astype(F32)
    for copy in own:
        copy.wait()
    pl.semaphore_wait(barrier, nz + nterm - 1)

    remote(label, label_p, hand_send.at[4], hand_recv.at[4], partner).start()
    for h in range(2):
        for d in far_first:
            remote(
                column[h].at[0],
                column[h].at[d],
                column_send.at[h],
                column_recv.at[h],
                on_z(d),
            ).start()
    load_left = pltpu.make_async_copy(left.at[0], left_v, local_sem.at[0])
    load_right = pltpu.make_async_copy(right.at[0], right_v, local_sem.at[1])
    load_left.start()
    load_right.start()

    def tag_row(which):
        row = label_p[8 * which : 8 * which + 1, :]
        return jnp.concatenate([row] * (wide // 128), axis=1)

    wait_for(label_p, hand_recv.at[4])

    def give(h):
        wait_for(column[h].at[other_z], column_recv.at[h])
        for which in range(2):
            wanted = tag_row(which)
            value = jnp.zeros((rows, wide), F32)
            for d in range(nz):
                here = (((z + d) % nz) * 2 + c).astype(F32)
                value = jnp.where(wanted == here, column[h][d].astype(F32), value)
            given[which, :, halves[h]] = value.astype(BF16)
            sem = 2 * which + h
            remote(
                given.at[which, :, halves[h]],
                handed.at[which, :, halves[h]],
                hand_send.at[sem],
                hand_recv.at[sem],
                partner,
            ).start()

    def place(which, h):
        wait_for(handed.at[which, :, halves[h]], hand_recv.at[2 * which + h])
        wanted = ends[which]
        local = column[h][(wanted // 2 + nz - z) % nz]
        blocks[which, my_rows, halves[h]] = jnp.where(
            wanted % 2 == c, local, handed[which, :, halves[h]]
        )
        to_all_terms(
            lambda j: remote(
                blocks.at[which, my_rows, halves[h]],
                blocks.at[which, my_rows, halves[h]],
                block_send.at[which, h],
                block_recv.at[which, h],
                on_term(j),
            )
        )

    give(0)
    place(0, 0)
    give(1)
    place(0, 1)
    place(1, 0)
    place(1, 1)

    def inner(which):
        for h in range(2):
            wait_for(blocks.at[which, other_rows, halves[h]], block_recv.at[which, h])

        def one(term, carry):
            active = jnp.where(mask_s[0, term] == 1, 1.0, 0.0).astype(F32)
            value = lax.dot_general(
                left_v[term],
                blocks[which],
                (((1 - which,), (0,)), ((), ())),
                preferred_element_type=F32,
            )
            inner_v[term] = (value * active).astype(BF16)
            return carry

        lax.fori_loop(0, terms, one, 0)

    def outer(which, h):
        value = jnp.zeros((order, wide), F32)
        for term in range(terms):
            operator = right_v[term, :, halves[h]] if which else right_v[term, halves[h], :]
            value = value + lax.dot_general(
                inner_v[term],
                operator,
                (((1,), (1 - which,)), ((), ())),
                preferred_element_type=F32,
            )
        total[which, :, halves[h]] = value
        part[which, :, halves[h]] = value.astype(BF16)
        to_all_terms(
            lambda j: remote(
                part.at[which, row_block((t + j) % nterm), halves[h]],
                arrived.at[which, nterm - 1 - j, :, halves[h]],
                part_send.at[which, h],
                part_recv.at[which, h],
                on_term(j),
            )
        )

    def reduce(which, h):
        wait_for(arrived.at[which, other_t, :, halves[h]], part_recv.at[which, h])
        value = total[which, my_rows, halves[h]]
        for j in range(nterm - 1):
            value = value + arrived[which, j, :, halves[h]].astype(F32)
        sums[which, :, halves[h]] = value.astype(BF16)
        remote(
            sums.at[which, :, halves[h]],
            sums_p.at[which, :, halves[h]],
            swap_send.at[which, h],
            swap_recv.at[which, h],
            partner,
        ).start()

    def swapped(which, h):
        wait_for(sums_p.at[which, :, halves[h]], swap_recv.at[which, h])

    def contribution(d, h):
        sector = ((z + nz - d) % nz) * 2 + c
        value = jnp.zeros((rows, wide), F32)
        for which in range(2):
            mine = jnp.where(ends[1 - which] == sector, 1.0, 0.0).astype(F32)
            value = value + sums[which, :, halves[h]].astype(F32) * mine
            theirs = tag_row(1 - which) == sector.astype(F32)
            value = value + jnp.where(theirs, sums_p[which, :, halves[h]].astype(F32), 0.0)
        return value.astype(BF16)

    def scatter(h):
        for d in far_first:
            leaving[d, :, halves[h]] = contribution(d, h)
            remote(
                leaving.at[d, :, halves[h]],
                landed.at[d, :, halves[h]],
                land_send.at[h],
                land_recv.at[h],
                on_z(d),
            ).start()

    keep = []

    def finish(h):
        value = contribution(0, h).astype(F32)
        wait_for(landed.at[other_z, :, halves[h]], land_recv.at[h])
        for d in range(1, nz):
            value = value + landed[d, :, halves[h]].astype(F32)
        mine_v[:, halves[h]] = value.astype(BF16)
        to_all_terms(
            lambda j: remote(
                mine_v.at[:, halves[h]],
                out.at[0, my_rows, halves[h]],
                out_send.at[h],
                out_recv.at[h],
                on_term(j),
            )
        )
        keep.append(
            pltpu.make_async_copy(
                mine_v.at[:, halves[h]], out.at[0, my_rows, halves[h]], local_sem.at[2 + h]
            )
        )
        keep[-1].start()

    load_left.wait()
    inner(0)
    load_right.wait()
    outer(0, 0)
    outer(0, 1)
    inner(1)
    reduce(0, 0)
    outer(1, 0)
    reduce(0, 1)
    outer(1, 1)
    swapped(0, 0)
    swapped(0, 1)
    reduce(1, 0)
    swapped(1, 0)
    scatter(0)
    reduce(1, 1)
    swapped(1, 1)
    scatter(1)
    finish(0)
    finish(1)

    wait_for(label, hand_send.at[4])
    for h in range(2):
        wait_for(column[h].at[other_z], column_send.at[h])
        wait_for(landed.at[other_z, :, halves[h]], land_send.at[h])
        for which in range(2):
            wait_for(given.at[which, :, halves[h]], hand_send.at[2 * which + h])
            wait_for(blocks.at[which, other_rows, halves[h]], block_send.at[which, h])
            wait_for(part.at[which, other_rows, halves[h]], part_send.at[which, h])
            wait_for(sums.at[which, :, halves[h]], swap_send.at[which, h])
        keep[h].wait()
        wait_for(out.at[0, other_rows, halves[h]], out_send.at[h])
        wait_for(out.at[0, other_rows, halves[h]], out_recv.at[h])


def solution(mesh):
    nsec, nterm = mesh.shape["sec"], mesh.shape["term"]
    placed = (
        P("sec", None, None),
        P("sec", "term", None, None),
        P("sec", "term", None, None),
        P("sec", "term"),
        P("sec"),
        P("sec"),
    )

    def local(psi, left_ops, right_ops, term_mask, pair_src, pair_dst):
        order, terms = psi.shape[1], left_ops.shape[1]
        rows, nz = order // nterm, nsec // 2
        anywhere = pl.BlockSpec(memory_space=pl.ANY)
        dma = pltpu.SemaphoreType.DMA
        return pl.pallas_call(
            functools.partial(kernel, (nsec, nterm, terms, order)),
            out_shape=jax.ShapeDtypeStruct(psi.shape, BF16),
            in_specs=[anywhere] * 6,
            out_specs=anywhere,
            scratch_shapes=[
                pltpu.VMEM((terms, order, order), BF16),
                pltpu.VMEM((terms, order, order), BF16),
                pltpu.VMEM((nz, rows, order // 2), BF16),
                pltpu.VMEM((nz, rows, order // 2), BF16),
                pltpu.VMEM((2, rows, order), BF16),
                pltpu.VMEM((2, rows, order), BF16),
                pltpu.VMEM((2, order, order), BF16),
                pltpu.VMEM((16, 128), F32),
                pltpu.VMEM((16, 128), F32),
                pltpu.VMEM((terms, order, order), BF16),
                pltpu.VMEM((2, order, order), F32),
                pltpu.VMEM((2, order, order), BF16),
                pltpu.VMEM((2, nterm, rows, order), BF16),
                pltpu.VMEM((2, rows, order), BF16),
                pltpu.VMEM((2, rows, order), BF16),
                pltpu.VMEM((nz, rows, order), BF16),
                pltpu.VMEM((nz, rows, order), BF16),
                pltpu.VMEM((rows, order), BF16),
                pltpu.SMEM((1, terms), jnp.int32),
                pltpu.SMEM((1,), jnp.int32),
                pltpu.SMEM((1,), jnp.int32),
                dma((6,)),
                dma((5,)),
                dma((5,)),
                dma((2,)),
                dma((2,)),
                dma((2, 2)),
                dma((2, 2)),
                dma((2, 2)),
                dma((2, 2)),
                dma((2, 2)),
                dma((2, 2)),
                dma((2,)),
                dma((2,)),
                dma((2,)),
                dma((2,)),
            ],
            compiler_params=pltpu.CompilerParams(
                collective_id=0, has_side_effects=True, vmem_limit_bytes=67043328
            ),
        )(psi, left_ops, right_ops, term_mask, pair_src, pair_dst)

    return jax.shard_map(
        local, mesh=mesh, in_specs=placed, out_specs=P("sec", None, None), check_vma=False
    )
```

```python
import functools

import jax
import jax.numpy as jnp
from jax import lax
from jax.experimental import pallas as pl
from jax.experimental.pallas import tpu as pltpu
from jax.sharding import PartitionSpec as P

MESH = pl.DeviceIdType.MESH
F32, BF16 = jnp.float32, jnp.bfloat16


def remote(src, dst, send_sem, recv_sem, device):
    return pltpu.make_async_remote_copy(
        src_ref=src,
        dst_ref=dst,
        send_sem=send_sem,
        recv_sem=recv_sem,
        device_id=device,
        device_id_type=MESH,
    )


def wait_for(ref, sem):
    pltpu.make_async_copy(ref, ref, sem).wait()


def kernel(
    sizes,
    psi,
    left,
    right,
    mask,
    src,
    dst,
    out,
    left_v,
    right_v,
    column_a,
    column_b,
    handed,
    given,
    blocks,
    label,
    label_p,
    inner_v,
    total,
    part,
    arrived,
    sums,
    sums_p,
    leaving,
    landed,
    mine_v,
    mask_s,
    src_s,
    dst_s,
    local_sem,
    hand_send,
    hand_recv,
    column_send,
    column_recv,
    block_send,
    block_recv,
    part_send,
    part_recv,
    swap_send,
    swap_recv,
    land_send,
    land_recv,
    out_send,
    out_recv,
):
    nsec, nterm, terms, order = sizes
    column = (column_a, column_b)
    nz = nsec // 2
    rows = order // nterm
    wide = order // 2
    s, t = lax.axis_index("sec"), lax.axis_index("term")
    z, c = s // 2, s % 2
    partner = {"sec": z * 2 + (1 - c)}
    halves = [pl.ds(h * wide, wide) for h in range(2)]
    other_z = pl.ds(1, nz - 1)
    other_t = pl.ds(0, nterm - 1)
    other_rows = pl.ds(0, (nterm - 1) * rows)

    def on_z(d):
        return {"sec": ((z + nz - d) % nz) * 2 + c}

    def on_term(j):
        return {"term": (t + j) % nterm}

    def row_block(index):
        return pl.ds(pl.multiple_of(index * rows, rows), rows)

    def to_all_terms(make):
        def start(j, carry):
            make(j).start()
            return carry

        lax.fori_loop(1, nterm, start, 0)

    my_rows = row_block(t)
    far_first = sorted(range(1, nz), key=lambda d: -min(d, nz - d))

    scalars = [
        pltpu.make_async_copy(a, b, local_sem.at[3 + i])
        for i, (a, b) in enumerate(((mask, mask_s), (src, src_s), (dst, dst_s)))
    ]
    for copy in scalars:
        copy.start()
    own = [
        pltpu.make_async_copy(psi.at[0, my_rows, halves[h]], column[h].at[0], local_sem.at[1 + h])
        for h in range(2)
    ]
    for copy in own:
        copy.start()

    barrier = pltpu.get_barrier_semaphore()
    for d in far_first:
        pl.semaphore_signal(barrier, inc=1, device_id=on_z(d), device_id_type=MESH)
    pl.semaphore_signal(barrier, inc=1, device_id=partner, device_id_type=MESH)

    def greet(j, carry):
        pl.semaphore_signal(barrier, inc=1, device_id=on_term(j), device_id_type=MESH)
        return carry

    lax.fori_loop(1, nterm, greet, 0)
    for copy in scalars:
        copy.wait()
    ends = (src_s[0], dst_s[0])
    for which in range(2):
        label[8 * which : 8 * which + 8, :] = jnp.full((8, 128), ends[which], jnp.int32).astype(F32)
    for copy in own:
        copy.wait()
    pl.semaphore_wait(barrier, nz + nterm - 1)

    load_left = pltpu.make_async_copy(left.at[0], left_v, local_sem.at[0])
    load_right = pltpu.make_async_copy(right.at[0], right_v, local_sem.at[1])

    remote(label, label_p, hand_send.at[4], hand_recv.at[4], partner).start()
    for h in range(2):
        if h == 1:
            wait_for(column[0].at[other_z], column_send.at[0])
        for d in far_first:
            remote(
                column[h].at[0],
                column[h].at[d],
                column_send.at[h],
                column_recv.at[h],
                on_z(d),
            ).start()
        if h == 0:
            load_left.start()
            load_right.start()

    def tag_row(which):
        row = label_p[8 * which : 8 * which + 1, :]
        return jnp.concatenate([row] * (wide // 128), axis=1)

    wait_for(label_p, hand_recv.at[4])

    def give(h):
        wait_for(column[h].at[other_z], column_recv.at[h])
        for which in range(2):
            wanted = tag_row(which)
            value = jnp.zeros((rows, wide), F32)
            for d in range(nz):
                here = (((z + d) % nz) * 2 + c).astype(F32)
                value = jnp.where(wanted == here, column[h][d].astype(F32), value)
            given[which, :, halves[h]] = value.astype(BF16)
            sem = 2 * which + h
            remote(
                given.at[which, :, halves[h]],
                handed.at[which, :, halves[h]],
                hand_send.at[sem],
                hand_recv.at[sem],
                partner,
            ).start()

    def place(which, h):
        wait_for(handed.at[which, :, halves[h]], hand_recv.at[2 * which + h])
        wanted = ends[which]
        local = column[h][(wanted // 2 + nz - z) % nz]
        blocks[which, my_rows, halves[h]] = jnp.where(
            wanted % 2 == c, local, handed[which, :, halves[h]]
        )
        to_all_terms(
            lambda j: remote(
                blocks.at[which, my_rows, halves[h]],
                blocks.at[which, my_rows, halves[h]],
                block_send.at[which, h],
                block_recv.at[which, h],
                on_term(j),
            )
        )

    give(0)
    place(0, 0)
    give(1)
    place(0, 1)
    wait_for(blocks.at[0, other_rows, halves[1]], block_send.at[0, 1])
    place(1, 0)
    place(1, 1)

    def inner(which):
        for h in range(2):
            wait_for(blocks.at[which, other_rows, halves[h]], block_recv.at[which, h])

        def one(term, carry):
            active = jnp.where(mask_s[0, term] == 1, 1.0, 0.0).astype(F32)
            value = lax.dot_general(
                left_v[term],
                blocks[which],
                (((1 - which,), (0,)), ((), ())),
                preferred_element_type=F32,
            )
            inner_v[term] = (value * active).astype(BF16)
            return carry

        lax.fori_loop(0, terms, one, 0)

    def outer(which, h):
        value = jnp.zeros((order, wide), F32)
        for term in range(terms):
            operator = right_v[term, :, halves[h]] if which else right_v[term, halves[h], :]
            value = value + lax.dot_general(
                inner_v[term],
                operator,
                (((1,), (1 - which,)), ((), ())),
                preferred_element_type=F32,
            )
        total[which, :, halves[h]] = value
        part[which, :, halves[h]] = value.astype(BF16)
        to_all_terms(
            lambda j: remote(
                part.at[which, row_block((t + j) % nterm), halves[h]],
                arrived.at[which, nterm - 1 - j, :, halves[h]],
                part_send.at[which, h],
                part_recv.at[which, h],
                on_term(j),
            )
        )

    def reduce(which, h):
        wait_for(arrived.at[which, other_t, :, halves[h]], part_recv.at[which, h])
        value = total[which, my_rows, halves[h]]
        for j in range(nterm - 1):
            value = value + arrived[which, j, :, halves[h]].astype(F32)
        sums[which, :, halves[h]] = value.astype(BF16)
        remote(
            sums.at[which, :, halves[h]],
            sums_p.at[which, :, halves[h]],
            swap_send.at[which, h],
            swap_recv.at[which, h],
            partner,
        ).start()

    def swapped(which, h):
        wait_for(sums_p.at[which, :, halves[h]], swap_recv.at[which, h])

    def contribution(d, h):
        sector = ((z + nz - d) % nz) * 2 + c
        value = jnp.zeros((rows, wide), F32)
        for which in range(2):
            mine = jnp.where(ends[1 - which] == sector, 1.0, 0.0).astype(F32)
            value = value + sums[which, :, halves[h]].astype(F32) * mine
            theirs = tag_row(1 - which) == sector.astype(F32)
            value = value + jnp.where(theirs, sums_p[which, :, halves[h]].astype(F32), 0.0)
        return value.astype(BF16)

    def scatter(h):
        for d in far_first:
            leaving[d, :, halves[h]] = contribution(d, h)
            remote(
                leaving.at[d, :, halves[h]],
                landed.at[d, :, halves[h]],
                land_send.at[h],
                land_recv.at[h],
                on_z(d),
            ).start()

    keep = []

    def finish(h):
        value = contribution(0, h).astype(F32)
        wait_for(landed.at[other_z, :, halves[h]], land_recv.at[h])
        for d in range(1, nz):
            value = value + landed[d, :, halves[h]].astype(F32)
        mine_v[:, halves[h]] = value.astype(BF16)
        to_all_terms(
            lambda j: remote(
                mine_v.at[:, halves[h]],
                out.at[0, my_rows, halves[h]],
                out_send.at[h],
                out_recv.at[h],
                on_term(j),
            )
        )
        keep.append(
            pltpu.make_async_copy(
                mine_v.at[:, halves[h]], out.at[0, my_rows, halves[h]], local_sem.at[2 + h]
            )
        )
        keep[-1].start()

    load_left.wait()
    inner(0)
    load_right.wait()
    outer(0, 0)
    outer(0, 1)
    inner(1)
    reduce(0, 0)
    outer(1, 0)
    reduce(0, 1)
    outer(1, 1)
    swapped(0, 0)
    swapped(0, 1)
    reduce(1, 0)
    swapped(1, 0)
    scatter(0)
    reduce(1, 1)
    swapped(1, 1)
    scatter(1)
    finish(0)
    finish(1)

    wait_for(label, hand_send.at[4])
    for h in range(2):
        if h == 1:
            wait_for(column[h].at[other_z], column_send.at[h])
        wait_for(landed.at[other_z, :, halves[h]], land_send.at[h])
        for which in range(2):
            wait_for(given.at[which, :, halves[h]], hand_send.at[2 * which + h])
            if (which, h) != (0, 1):
                wait_for(blocks.at[which, other_rows, halves[h]], block_send.at[which, h])
            wait_for(part.at[which, other_rows, halves[h]], part_send.at[which, h])
            wait_for(sums.at[which, :, halves[h]], swap_send.at[which, h])
        keep[h].wait()
        wait_for(out.at[0, other_rows, halves[h]], out_send.at[h])
        wait_for(out.at[0, other_rows, halves[h]], out_recv.at[h])


def solution(mesh):
    nsec, nterm = mesh.shape["sec"], mesh.shape["term"]
    placed = (
        P("sec", None, None),
        P("sec", "term", None, None),
        P("sec", "term", None, None),
        P("sec", "term"),
        P("sec"),
        P("sec"),
    )

    def local(psi, left_ops, right_ops, term_mask, pair_src, pair_dst):
        order, terms = psi.shape[1], left_ops.shape[1]
        rows, nz = order // nterm, nsec // 2
        anywhere = pl.BlockSpec(memory_space=pl.ANY)
        dma = pltpu.SemaphoreType.DMA
        return pl.pallas_call(
            functools.partial(kernel, (nsec, nterm, terms, order)),
            out_shape=jax.ShapeDtypeStruct(psi.shape, BF16),
            in_specs=[anywhere] * 6,
            out_specs=anywhere,
            scratch_shapes=[
                pltpu.VMEM((terms, order, order), BF16),
                pltpu.VMEM((terms, order, order), BF16),
                pltpu.VMEM((nz, rows, order // 2), BF16),
                pltpu.VMEM((nz, rows, order // 2), BF16),
                pltpu.VMEM((2, rows, order), BF16),
                pltpu.VMEM((2, rows, order), BF16),
                pltpu.VMEM((2, order, order), BF16),
                pltpu.VMEM((16, 128), F32),
                pltpu.VMEM((16, 128), F32),
                pltpu.VMEM((terms, order, order), BF16),
                pltpu.VMEM((2, order, order), F32),
                pltpu.VMEM((2, order, order), BF16),
                pltpu.VMEM((2, nterm, rows, order), BF16),
                pltpu.VMEM((2, rows, order), BF16),
                pltpu.VMEM((2, rows, order), BF16),
                pltpu.VMEM((nz, rows, order), BF16),
                pltpu.VMEM((nz, rows, order), BF16),
                pltpu.VMEM((rows, order), BF16),
                pltpu.SMEM((1, terms), jnp.int32),
                pltpu.SMEM((1,), jnp.int32),
                pltpu.SMEM((1,), jnp.int32),
                dma((6,)),
                dma((5,)),
                dma((5,)),
                dma((2,)),
                dma((2,)),
                dma((2, 2)),
                dma((2, 2)),
                dma((2, 2)),
                dma((2, 2)),
                dma((2, 2)),
                dma((2, 2)),
                dma((2,)),
                dma((2,)),
                dma((2,)),
                dma((2,)),
            ],
            compiler_params=pltpu.CompilerParams(
                collective_id=0, has_side_effects=True, vmem_limit_bytes=67043328
            ),
        )(psi, left_ops, right_ops, term_mask, pair_src, pair_dst)

    return jax.shard_map(
        local, mesh=mesh, in_specs=placed, out_specs=P("sec", None, None), check_vma=False
    )
```

```python
import functools

import jax
import jax.numpy as jnp
from jax import lax
from jax.experimental import pallas as pl
from jax.experimental.pallas import tpu as pltpu
from jax.sharding import PartitionSpec as P

MESH = pl.DeviceIdType.MESH
F32, BF16 = jnp.float32, jnp.bfloat16


def remote(src, dst, send_sem, recv_sem, device):
    return pltpu.make_async_remote_copy(
        src_ref=src,
        dst_ref=dst,
        send_sem=send_sem,
        recv_sem=recv_sem,
        device_id=device,
        device_id_type=MESH,
    )


def wait_for(ref, sem):
    pltpu.make_async_copy(ref, ref, sem).wait()


def kernel(
    sizes,
    psi,
    left,
    right,
    mask,
    src,
    dst,
    out,
    left_v,
    right_v,
    column_a,
    column_b,
    handed,
    given,
    blocks,
    label,
    label_p,
    inner_v,
    total,
    part,
    arrived,
    sums,
    sums_p,
    leaving,
    landed,
    mine_v,
    mask_s,
    src_s,
    dst_s,
    local_sem,
    hand_send,
    hand_recv,
    column_send,
    column_recv,
    block_send,
    block_recv,
    part_send,
    part_recv,
    swap_send,
    swap_recv,
    land_send,
    land_recv,
    out_send,
    out_recv,
):
    nsec, nterm, terms, order = sizes
    column = (column_a, column_b)
    nz = nsec // 2
    rows = order // nterm
    wide = order // 2
    s, t = lax.axis_index("sec"), lax.axis_index("term")
    z, c = s // 2, s % 2
    partner = {"sec": z * 2 + (1 - c)}
    halves = [pl.ds(h * wide, wide) for h in range(2)]
    other_z = pl.ds(1, nz - 1)
    other_t = pl.ds(0, nterm - 1)
    other_rows = pl.ds(0, (nterm - 1) * rows)

    def on_z(d):
        return {"sec": ((z + nz - d) % nz) * 2 + c}

    def on_term(j):
        return {"term": (t + j) % nterm}

    def row_block(index):
        return pl.ds(pl.multiple_of(index * rows, rows), rows)

    def to_all_terms(make):
        def start(j, carry):
            make(j).start()
            return carry

        lax.fori_loop(1, nterm, start, 0)

    my_rows = row_block(t)
    far_first = sorted(range(1, nz), key=lambda d: -min(d, nz - d))

    scalars = [
        pltpu.make_async_copy(a, b, local_sem.at[3 + i])
        for i, (a, b) in enumerate(((mask, mask_s), (src, src_s), (dst, dst_s)))
    ]
    for copy in scalars:
        copy.start()
    own = [
        pltpu.make_async_copy(psi.at[0, my_rows, halves[h]], column[h].at[0], local_sem.at[1 + h])
        for h in range(2)
    ]
    for copy in own:
        copy.start()

    barrier = pltpu.get_barrier_semaphore()
    for d in far_first:
        pl.semaphore_signal(barrier, inc=1, device_id=on_z(d), device_id_type=MESH)
    pl.semaphore_signal(barrier, inc=1, device_id=partner, device_id_type=MESH)

    def greet(j, carry):
        pl.semaphore_signal(barrier, inc=1, device_id=on_term(j), device_id_type=MESH)
        return carry

    lax.fori_loop(1, nterm, greet, 0)
    for copy in scalars:
        copy.wait()
    ends = (src_s[0], dst_s[0])
    for which in range(2):
        label[8 * which : 8 * which + 8, :] = jnp.full((8, 128), ends[which], jnp.int32).astype(F32)
    for copy in own:
        copy.wait()
    pl.semaphore_wait(barrier, nz + nterm - 1)

    load_left = pltpu.make_async_copy(left.at[0], left_v, local_sem.at[0])
    load_right = pltpu.make_async_copy(right.at[0], right_v, local_sem.at[1])

    remote(label, label_p, hand_send.at[4], hand_recv.at[4], partner).start()
    for h in range(2):
        if h == 1:
            wait_for(column[0].at[other_z], column_send.at[0])
        for d in far_first:
            remote(
                column[h].at[0],
                column[h].at[d],
                column_send.at[h],
                column_recv.at[h],
                on_z(d),
            ).start()
        if h == 0:
            load_left.start()
            load_right.start()

    def tag_row(which):
        row = label_p[8 * which : 8 * which + 1, :]
        return jnp.concatenate([row] * (wide // 128), axis=1)

    wait_for(label_p, hand_recv.at[4])

    def give(h):
        wait_for(column[h].at[other_z], column_recv.at[h])
        for which in range(2):
            wanted = tag_row(which)
            value = jnp.zeros((rows, wide), F32)
            for d in range(nz):
                here = (((z + d) % nz) * 2 + c).astype(F32)
                value = jnp.where(wanted == here, column[h][d].astype(F32), value)
            given[which, :, halves[h]] = value.astype(BF16)
            sem = 2 * which + h
            remote(
                given.at[which, :, halves[h]],
                handed.at[which, :, halves[h]],
                hand_send.at[sem],
                hand_recv.at[sem],
                partner,
            ).start()

    def place(which, h):
        wait_for(handed.at[which, :, halves[h]], hand_recv.at[2 * which + h])
        wanted = ends[which]
        local = column[h][(wanted // 2 + nz - z) % nz]
        blocks[which, my_rows, halves[h]] = jnp.where(
            wanted % 2 == c, local, handed[which, :, halves[h]]
        )
        to_all_terms(
            lambda j: remote(
                blocks.at[which, my_rows, halves[h]],
                blocks.at[which, my_rows, halves[h]],
                block_send.at[which, h],
                block_recv.at[which, h],
                on_term(j),
            )
        )

    give(0)
    place(0, 0)
    give(1)
    place(0, 1)
    wait_for(blocks.at[0, other_rows, halves[1]], block_send.at[0, 1])
    place(1, 0)
    place(1, 1)

    def inner(which):
        for h in range(2):
            wait_for(blocks.at[which, other_rows, halves[h]], block_recv.at[which, h])

        def one(term, carry):
            active = jnp.where(mask_s[0, term] == 1, 1.0, 0.0).astype(F32)
            value = lax.dot_general(
                left_v[term],
                blocks[which],
                (((1 - which,), (0,)), ((), ())),
                preferred_element_type=F32,
            )
            inner_v[term] = (value * active).astype(BF16)
            return carry

        lax.fori_loop(0, terms, one, 0)

    def outer(which, h):
        value = jnp.zeros((order, wide), F32)
        for term in range(terms):
            operator = right_v[term, :, halves[h]] if which else right_v[term, halves[h], :]
            value = value + lax.dot_general(
                inner_v[term],
                operator,
                (((1,), (1 - which,)), ((), ())),
                preferred_element_type=F32,
            )
        total[which, :, halves[h]] = value
        part[which, :, halves[h]] = value.astype(BF16)
        to_all_terms(
            lambda j: remote(
                part.at[which, row_block((t + j) % nterm), halves[h]],
                arrived.at[which, nterm - 1 - j, :, halves[h]],
                part_send.at[which, h],
                part_recv.at[which, h],
                on_term(j),
            )
        )

    def reduce(which, h):
        wait_for(arrived.at[which, other_t, :, halves[h]], part_recv.at[which, h])
        value = total[which, my_rows, halves[h]]
        for j in range(nterm - 1):
            value = value + arrived[which, j, :, halves[h]].astype(F32)
        sums[which, :, halves[h]] = value.astype(BF16)
        remote(
            sums.at[which, :, halves[h]],
            sums_p.at[which, :, halves[h]],
            swap_send.at[which, h],
            swap_recv.at[which, h],
            partner,
        ).start()

    def swapped(which, h):
        wait_for(sums_p.at[which, :, halves[h]], swap_recv.at[which, h])

    def contribution(d, h):
        sector = ((z + nz - d) % nz) * 2 + c
        value = jnp.zeros((rows, wide), F32)
        for which in range(2):
            mine = jnp.where(ends[1 - which] == sector, 1.0, 0.0).astype(F32)
            value = value + sums[which, :, halves[h]].astype(F32) * mine
            theirs = tag_row(1 - which) == sector.astype(F32)
            value = value + jnp.where(theirs, sums_p[which, :, halves[h]].astype(F32), 0.0)
        return value.astype(BF16)

    def scatter(h):
        for d in far_first:
            leaving[d, :, halves[h]] = contribution(d, h)
            remote(
                leaving.at[d, :, halves[h]],
                landed.at[d, :, halves[h]],
                land_send.at[h],
                land_recv.at[h],
                on_z(d),
            ).start()

    keep = []

    def finish(h):
        value = contribution(0, h).astype(F32)
        wait_for(landed.at[other_z, :, halves[h]], land_recv.at[h])
        for d in range(1, nz):
            value = value + landed[d, :, halves[h]].astype(F32)
        mine_v[:, halves[h]] = value.astype(BF16)
        to_all_terms(
            lambda j: remote(
                mine_v.at[:, halves[h]],
                out.at[0, my_rows, halves[h]],
                out_send.at[h],
                out_recv.at[h],
                on_term(j),
            )
        )
        keep.append(
            pltpu.make_async_copy(
                mine_v.at[:, halves[h]], out.at[0, my_rows, halves[h]], local_sem.at[2 + h]
            )
        )
        keep[-1].start()

    load_left.wait()
    inner(0)
    load_right.wait()
    outer(0, 0)
    outer(0, 1)
    inner(1)
    outer(1, 0)
    outer(1, 1)
    reduce(0, 0)
    reduce(0, 1)
    swapped(0, 0)
    swapped(0, 1)
    reduce(1, 0)
    swapped(1, 0)
    scatter(0)
    reduce(1, 1)
    swapped(1, 1)
    scatter(1)
    finish(0)
    finish(1)

    wait_for(label, hand_send.at[4])
    for h in range(2):
        if h == 1:
            wait_for(column[h].at[other_z], column_send.at[h])
        wait_for(landed.at[other_z, :, halves[h]], land_send.at[h])
        for which in range(2):
            wait_for(given.at[which, :, halves[h]], hand_send.at[2 * which + h])
            if (which, h) != (0, 1):
                wait_for(blocks.at[which, other_rows, halves[h]], block_send.at[which, h])
            wait_for(part.at[which, other_rows, halves[h]], part_send.at[which, h])
            wait_for(sums.at[which, :, halves[h]], swap_send.at[which, h])
        keep[h].wait()
        wait_for(out.at[0, other_rows, halves[h]], out_send.at[h])
        wait_for(out.at[0, other_rows, halves[h]], out_recv.at[h])


def solution(mesh):
    nsec, nterm = mesh.shape["sec"], mesh.shape["term"]
    placed = (
        P("sec", None, None),
        P("sec", "term", None, None),
        P("sec", "term", None, None),
        P("sec", "term"),
        P("sec"),
        P("sec"),
    )

    def local(psi, left_ops, right_ops, term_mask, pair_src, pair_dst):
        order, terms = psi.shape[1], left_ops.shape[1]
        rows, nz = order // nterm, nsec // 2
        anywhere = pl.BlockSpec(memory_space=pl.ANY)
        dma = pltpu.SemaphoreType.DMA
        return pl.pallas_call(
            functools.partial(kernel, (nsec, nterm, terms, order)),
            out_shape=jax.ShapeDtypeStruct(psi.shape, BF16),
            in_specs=[anywhere] * 6,
            out_specs=anywhere,
            scratch_shapes=[
                pltpu.VMEM((terms, order, order), BF16),
                pltpu.VMEM((terms, order, order), BF16),
                pltpu.VMEM((nz, rows, order // 2), BF16),
                pltpu.VMEM((nz, rows, order // 2), BF16),
                pltpu.VMEM((2, rows, order), BF16),
                pltpu.VMEM((2, rows, order), BF16),
                pltpu.VMEM((2, order, order), BF16),
                pltpu.VMEM((16, 128), F32),
                pltpu.VMEM((16, 128), F32),
                pltpu.VMEM((terms, order, order), BF16),
                pltpu.VMEM((2, order, order), F32),
                pltpu.VMEM((2, order, order), BF16),
                pltpu.VMEM((2, nterm, rows, order), BF16),
                pltpu.VMEM((2, rows, order), BF16),
                pltpu.VMEM((2, rows, order), BF16),
                pltpu.VMEM((nz, rows, order), BF16),
                pltpu.VMEM((nz, rows, order), BF16),
                pltpu.VMEM((rows, order), BF16),
                pltpu.SMEM((1, terms), jnp.int32),
                pltpu.SMEM((1,), jnp.int32),
                pltpu.SMEM((1,), jnp.int32),
                dma((6,)),
                dma((5,)),
                dma((5,)),
                dma((2,)),
                dma((2,)),
                dma((2, 2)),
                dma((2, 2)),
                dma((2, 2)),
                dma((2, 2)),
                dma((2, 2)),
                dma((2, 2)),
                dma((2,)),
                dma((2,)),
                dma((2,)),
                dma((2,)),
            ],
            compiler_params=pltpu.CompilerParams(
                collective_id=0, has_side_effects=True, vmem_limit_bytes=67043328
            ),
        )(psi, left_ops, right_ops, term_mask, pair_src, pair_dst)

    return jax.shard_map(
        local, mesh=mesh, in_specs=placed, out_specs=P("sec", None, None), check_vma=False
    )
```

```python
import functools

import jax
import jax.numpy as jnp
from jax import lax
from jax.experimental import pallas as pl
from jax.experimental.pallas import tpu as pltpu
from jax.sharding import PartitionSpec as P

MESH = pl.DeviceIdType.MESH
F32, BF16 = jnp.float32, jnp.bfloat16


def remote(src, dst, send_sem, recv_sem, device):
    return pltpu.make_async_remote_copy(
        src_ref=src,
        dst_ref=dst,
        send_sem=send_sem,
        recv_sem=recv_sem,
        device_id=device,
        device_id_type=MESH,
    )


def wait_for(ref, sem):
    pltpu.make_async_copy(ref, ref, sem).wait()


def kernel(
    sizes,
    psi,
    left,
    right,
    mask,
    src,
    dst,
    out,
    left_v,
    right_v,
    column_a,
    column_b,
    handed,
    given,
    blocks,
    label,
    label_p,
    inner_v,
    total,
    part,
    arrived,
    sums,
    sums_p,
    leaving,
    landed,
    mine_v,
    mask_s,
    src_s,
    dst_s,
    local_sem,
    hand_send,
    hand_recv,
    column_send,
    column_recv,
    block_send,
    block_recv,
    part_send,
    part_recv,
    swap_send,
    swap_recv,
    land_send,
    land_recv,
    out_send,
    out_recv,
):
    nsec, nterm, terms, order = sizes
    column = (column_a, column_b)
    nz = nsec // 2
    rows = order // nterm
    wide = order // 2
    s, t = lax.axis_index("sec"), lax.axis_index("term")
    z, c = s // 2, s % 2
    partner = {"sec": z * 2 + (1 - c)}
    halves = [pl.ds(h * wide, wide) for h in range(2)]
    other_z = pl.ds(1, nz - 1)
    other_t = pl.ds(0, nterm - 1)
    other_rows = pl.ds(0, (nterm - 1) * rows)

    def on_z(d):
        return {"sec": ((z + nz - d) % nz) * 2 + c}

    def on_term(j):
        return {"term": (t + j) % nterm}

    def row_block(index):
        return pl.ds(pl.multiple_of(index * rows, rows), rows)

    def to_all_terms(make):
        def start(j, carry):
            make(j).start()
            return carry

        lax.fori_loop(1, nterm, start, 0)

    my_rows = row_block(t)
    far_first = sorted(range(1, nz), key=lambda d: -min(d, nz - d))

    scalars = [
        pltpu.make_async_copy(a, b, local_sem.at[3 + i])
        for i, (a, b) in enumerate(((mask, mask_s), (src, src_s), (dst, dst_s)))
    ]
    for copy in scalars:
        copy.start()
    own = [
        pltpu.make_async_copy(psi.at[0, my_rows, halves[h]], column[h].at[0], local_sem.at[1 + h])
        for h in range(2)
    ]
    for copy in own:
        copy.start()

    barrier = pltpu.get_barrier_semaphore()
    for d in far_first:
        pl.semaphore_signal(barrier, inc=1, device_id=on_z(d), device_id_type=MESH)
    pl.semaphore_signal(barrier, inc=1, device_id=partner, device_id_type=MESH)

    def greet(j, carry):
        pl.semaphore_signal(barrier, inc=1, device_id=on_term(j), device_id_type=MESH)
        return carry

    lax.fori_loop(1, nterm, greet, 0)
    for copy in scalars:
        copy.wait()
    ends = (src_s[0], dst_s[0])
    for which in range(2):
        label[8 * which : 8 * which + 8, :] = jnp.full((8, 128), ends[which], jnp.int32).astype(F32)
    for copy in own:
        copy.wait()
    pl.semaphore_wait(barrier, nz + nterm - 1)

    load_left = pltpu.make_async_copy(left.at[0], left_v, local_sem.at[0])
    load_right = pltpu.make_async_copy(right.at[0], right_v, local_sem.at[1])

    remote(label, label_p, hand_send.at[4], hand_recv.at[4], partner).start()
    for h in range(2):
        if h == 1:
            wait_for(column[0].at[other_z], column_send.at[0])
        for d in far_first:
            remote(
                column[h].at[0],
                column[h].at[d],
                column_send.at[h],
                column_recv.at[h],
                on_z(d),
            ).start()
        if h == 0:
            load_left.start()
            load_right.start()

    def tag_row(which):
        row = label_p[8 * which : 8 * which + 1, :]
        return jnp.concatenate([row] * (wide // 128), axis=1)

    wait_for(label_p, hand_recv.at[4])

    def give(h):
        wait_for(column[h].at[other_z], column_recv.at[h])
        for which in range(2):
            wanted = tag_row(which)
            value = jnp.zeros((rows, wide), F32)
            for d in range(nz):
                here = (((z + d) % nz) * 2 + c).astype(F32)
                value = jnp.where(wanted == here, column[h][d].astype(F32), value)
            given[which, :, halves[h]] = value.astype(BF16)
            sem = 2 * which + h
            remote(
                given.at[which, :, halves[h]],
                handed.at[which, :, halves[h]],
                hand_send.at[sem],
                hand_recv.at[sem],
                partner,
            ).start()

    def place(which, h):
        wait_for(handed.at[which, :, halves[h]], hand_recv.at[2 * which + h])
        wanted = ends[which]
        local = column[h][(wanted // 2 + nz - z) % nz]
        blocks[which, my_rows, halves[h]] = jnp.where(
            wanted % 2 == c, local, handed[which, :, halves[h]]
        )
        to_all_terms(
            lambda j: remote(
                blocks.at[which, my_rows, halves[h]],
                blocks.at[which, my_rows, halves[h]],
                block_send.at[which, h],
                block_recv.at[which, h],
                on_term(j),
            )
        )

    give(0)
    place(0, 0)
    give(1)
    place(0, 1)
    wait_for(blocks.at[0, other_rows, halves[0]], block_send.at[0, 0])
    place(1, 0)
    place(1, 1)

    def inner(which):
        for h in range(2):
            wait_for(blocks.at[which, other_rows, halves[h]], block_recv.at[which, h])

        def one(term, carry):
            active = jnp.where(mask_s[0, term] == 1, 1.0, 0.0).astype(F32)
            value = lax.dot_general(
                left_v[term],
                blocks[which],
                (((1 - which,), (0,)), ((), ())),
                preferred_element_type=F32,
            )
            inner_v[term] = (value * active).astype(BF16)
            return carry

        lax.fori_loop(0, terms, one, 0)

    def outer(which, h):
        value = jnp.zeros((order, wide), F32)
        for term in range(terms):
            operator = right_v[term, :, halves[h]] if which else right_v[term, halves[h], :]
            value = value + lax.dot_general(
                inner_v[term],
                operator,
                (((1,), (1 - which,)), ((), ())),
                preferred_element_type=F32,
            )
        total[which, :, halves[h]] = value
        part[which, :, halves[h]] = value.astype(BF16)
        to_all_terms(
            lambda j: remote(
                part.at[which, row_block((t + j) % nterm), halves[h]],
                arrived.at[which, nterm - 1 - j, :, halves[h]],
                part_send.at[which, h],
                part_recv.at[which, h],
                on_term(j),
            )
        )

    def reduce(which, h):
        wait_for(arrived.at[which, other_t, :, halves[h]], part_recv.at[which, h])
        value = total[which, my_rows, halves[h]]
        for j in range(nterm - 1):
            value = value + arrived[which, j, :, halves[h]].astype(F32)
        sums[which, :, halves[h]] = value.astype(BF16)
        remote(
            sums.at[which, :, halves[h]],
            sums_p.at[which, :, halves[h]],
            swap_send.at[which, h],
            swap_recv.at[which, h],
            partner,
        ).start()

    def swapped(which, h):
        wait_for(sums_p.at[which, :, halves[h]], swap_recv.at[which, h])

    def contribution(d, h):
        sector = ((z + nz - d) % nz) * 2 + c
        value = jnp.zeros((rows, wide), F32)
        for which in range(2):
            mine = jnp.where(ends[1 - which] == sector, 1.0, 0.0).astype(F32)
            value = value + sums[which, :, halves[h]].astype(F32) * mine
            theirs = tag_row(1 - which) == sector.astype(F32)
            value = value + jnp.where(theirs, sums_p[which, :, halves[h]].astype(F32), 0.0)
        return value.astype(BF16)

    def scatter(h):
        for d in far_first:
            leaving[d, :, halves[h]] = contribution(d, h)
            remote(
                leaving.at[d, :, halves[h]],
                landed.at[d, :, halves[h]],
                land_send.at[h],
                land_recv.at[h],
                on_z(d),
            ).start()

    keep = []

    def finish(h):
        value = contribution(0, h).astype(F32)
        wait_for(landed.at[other_z, :, halves[h]], land_recv.at[h])
        for d in range(1, nz):
            value = value + landed[d, :, halves[h]].astype(F32)
        mine_v[:, halves[h]] = value.astype(BF16)
        to_all_terms(
            lambda j: remote(
                mine_v.at[:, halves[h]],
                out.at[0, my_rows, halves[h]],
                out_send.at[h],
                out_recv.at[h],
                on_term(j),
            )
        )
        keep.append(
            pltpu.make_async_copy(
                mine_v.at[:, halves[h]], out.at[0, my_rows, halves[h]], local_sem.at[2 + h]
            )
        )
        keep[-1].start()

    load_left.wait()
    inner(0)
    load_right.wait()
    outer(0, 0)
    outer(0, 1)
    inner(1)
    outer(1, 0)
    outer(1, 1)
    reduce(0, 0)
    reduce(0, 1)
    swapped(0, 0)
    swapped(0, 1)
    reduce(1, 0)
    swapped(1, 0)
    scatter(0)
    reduce(1, 1)
    swapped(1, 1)
    scatter(1)
    finish(0)
    finish(1)

    wait_for(label, hand_send.at[4])
    for h in range(2):
        if h == 1:
            wait_for(column[h].at[other_z], column_send.at[h])
        wait_for(landed.at[other_z, :, halves[h]], land_send.at[h])
        for which in range(2):
            wait_for(given.at[which, :, halves[h]], hand_send.at[2 * which + h])
            if (which, h) != (0, 0):
                wait_for(blocks.at[which, other_rows, halves[h]], block_send.at[which, h])
            wait_for(part.at[which, other_rows, halves[h]], part_send.at[which, h])
            wait_for(sums.at[which, :, halves[h]], swap_send.at[which, h])
        keep[h].wait()
        wait_for(out.at[0, other_rows, halves[h]], out_send.at[h])
        wait_for(out.at[0, other_rows, halves[h]], out_recv.at[h])


def solution(mesh):
    nsec, nterm = mesh.shape["sec"], mesh.shape["term"]
    placed = (
        P("sec", None, None),
        P("sec", "term", None, None),
        P("sec", "term", None, None),
        P("sec", "term"),
        P("sec"),
        P("sec"),
    )

    def local(psi, left_ops, right_ops, term_mask, pair_src, pair_dst):
        order, terms = psi.shape[1], left_ops.shape[1]
        rows, nz = order // nterm, nsec // 2
        anywhere = pl.BlockSpec(memory_space=pl.ANY)
        dma = pltpu.SemaphoreType.DMA
        return pl.pallas_call(
            functools.partial(kernel, (nsec, nterm, terms, order)),
            out_shape=jax.ShapeDtypeStruct(psi.shape, BF16),
            in_specs=[anywhere] * 6,
            out_specs=anywhere,
            scratch_shapes=[
                pltpu.VMEM((terms, order, order), BF16),
                pltpu.VMEM((terms, order, order), BF16),
                pltpu.VMEM((nz, rows, order // 2), BF16),
                pltpu.VMEM((nz, rows, order // 2), BF16),
                pltpu.VMEM((2, rows, order), BF16),
                pltpu.VMEM((2, rows, order), BF16),
                pltpu.VMEM((2, order, order), BF16),
                pltpu.VMEM((16, 128), F32),
                pltpu.VMEM((16, 128), F32),
                pltpu.VMEM((terms, order, order), BF16),
                pltpu.VMEM((2, order, order), F32),
                pltpu.VMEM((2, order, order), BF16),
                pltpu.VMEM((2, nterm, rows, order), BF16),
                pltpu.VMEM((2, rows, order), BF16),
                pltpu.VMEM((2, rows, order), BF16),
                pltpu.VMEM((nz, rows, order), BF16),
                pltpu.VMEM((nz, rows, order), BF16),
                pltpu.VMEM((rows, order), BF16),
                pltpu.SMEM((1, terms), jnp.int32),
                pltpu.SMEM((1,), jnp.int32),
                pltpu.SMEM((1,), jnp.int32),
                dma((6,)),
                dma((5,)),
                dma((5,)),
                dma((2,)),
                dma((2,)),
                dma((2, 2)),
                dma((2, 2)),
                dma((2, 2)),
                dma((2, 2)),
                dma((2, 2)),
                dma((2, 2)),
                dma((2,)),
                dma((2,)),
                dma((2,)),
                dma((2,)),
            ],
            compiler_params=pltpu.CompilerParams(
                collective_id=0, has_side_effects=True, vmem_limit_bytes=67043328
            ),
        )(psi, left_ops, right_ops, term_mask, pair_src, pair_dst)

    return jax.shard_map(
        local, mesh=mesh, in_specs=placed, out_specs=P("sec", None, None), check_vma=False
    )
```
